32 devices in a mesh: leaf: 4 (over x, core), front: 8 (over z, y).
Axes of the slice: x: 2, y: 2, z: 4, core: 2. Of those that a mesh axis runs over, the one named last changes fastest.
Arguments:
- leaf_field: float32 [64, 128, 4, 128], P(None, ('leaf', 'front')), may hold values from -4 to 4
- leaf_source: float32 [64, 128, 4, 128], P(None, ('leaf', 'front')), may hold values from -6 to 6
- wave_squared: float32 [128, 4, 128], P(('leaf', 'front')), may hold values from 0.5 to 3
- coupling_map: int32 [32, 512], P(('leaf', 'front')), may hold values from 0 to 255
- front_rhs: float32 [64, 2048], P(None, 'front'), may hold values from -6 to 6
- row_order: int32 [2048], P('front'), may hold values from 0 to 2047, each once
- lower_panels: bfloat16 [2048, 2048], P(None, 'front'), may hold values from -0.125 to 0.125
- inverse_slots: float32 [4096, 512], P('front'), as said below
- panel_owners: int32 [4], replicated, may hold values from 0 to 7, as said below
Outputs:
- leaf_residual: float32 [64, 128, 4, 128], P(None, ('leaf', 'front'))
- solved_blocks: float32 [64, 2048], replicated
- reduced_rhs: float32 [64, 2048], P(None, 'front')
The draws below stay inside these ranges and needn't reach their ends.
Inputs may be any that keep to these rules, and one draw needn't show every extreme that they name: `panel_owners`: 4 distinct indices of the front axis, always including 0 and 7. `inverse_slots`: each slot of 512 rows is lower triangular with diagonal entries between 0.5 and 1.5.
All inputs are finite; a program needn't handle non-finite values.
Results may differ from the reference program's by a relative error of at most 0.0019.
Values sent between devices are 32-bit elements; how exact they have to be, the bound alone decides.
No kernel may reach another device: no remote copies, remote signals or barrier semaphores. Data moves between devices by JAX's collectives and lax.ppermute only.
A program may use at most 64 MiB of HBM per device.

```python
import math
import jax
import jax.numpy as jnp
from jax import lax

NRHS = 64
PW = 512
PANELS = 4
ROWS_DEV = 256
GX = 4
GY = 4
GZ = 128
W = 2048
ROWS = 2048
BLOCKS = 8
SUBS = 32
FACE = 512


def draw_inverse_slots(key, part):
    key_diag, key_noise = jax.random.split(key)
    total = BLOCKS * PW
    diagonal = jax.random.uniform(key_diag, (total,), jnp.float32, 0.5, 1.5)
    noise = 0.8 * jax.random.normal(key_noise, (total, PW), jnp.float32) / math.sqrt(PW)
    row_index = jnp.arange(total, dtype=jnp.int32) % PW
    col_index = jnp.arange(PW, dtype=jnp.int32)
    lower = col_index[None, :] < row_index[:, None]
    on_diag = col_index[None, :] == row_index[:, None]
    result = jnp.where(on_diag, diagonal[:, None], jnp.where(lower, noise, 0.0))
    return result.astype(jnp.float32)


def draw_panel_owners(key, part):
    key_middle = jax.random.fold_in(key, 11)
    key_order = jax.random.fold_in(key, 23)
    middle = 1 + jax.random.permutation(key_middle, jnp.arange(BLOCKS - 2, dtype=jnp.int32))[:PANELS - 2]
    chosen = jnp.concatenate([jnp.array([0, BLOCKS - 1], dtype=jnp.int32), middle.astype(jnp.int32)])
    order = jax.random.permutation(key_order, jnp.arange(PANELS, dtype=jnp.int32))
    return chosen[order].astype(jnp.int32)


def place_ends(values, stream_key, least, largest):
    shape = values.shape
    place = [jax.random.randint(jax.random.fold_in(stream_key, axis), (), 0, shape[axis]) for axis in range(len(shape))]
    values = values.at[tuple(place)].set(least)
    longest = shape.index(max(shape))
    place[longest] = (place[longest] + 1) % shape[longest]
    return values.at[tuple(place)].set(largest)


def steps_of(rng, extent, cuts, low, high):
    level, own = 1.0, jax.random.fold_in(rng, 6)
    for axis_at, shards_of in cuts:
        draws = jnp.exp(jax.random.uniform(jax.random.fold_in(own, axis_at), (shards_of,), jnp.float32, low / len(cuts), high / len(cuts)))
        level = level * jnp.repeat(draws, extent[axis_at] // shards_of).reshape([-1 if axis == axis_at else 1 for axis in range(len(extent))])
    return level


def gaussian(stream_key, dims, width, reach, pieces=(), kind=jnp.bfloat16):
    factor_of = steps_of(stream_key, dims, pieces, -0.22, 0.18) if pieces else 1.0
    values = jax.random.normal(stream_key, dims, jnp.float32) * width * factor_of
    return jnp.minimum(jnp.maximum(values, -reach), reach).astype(kind)


def setup_inputs(seed: int = 0) -> dict:
    splits = jax.random.split(jax.random.key(seed), 10)
    leaf_field = gaussian(splits[0], (NRHS, SUBS * GX, GY, GZ), 0.25, 4.0, ((1, 32),), jnp.float32)
    leaf_source = gaussian(splits[1], (NRHS, SUBS * GX, GY, GZ), 0.5, 6.0, ((1, 32),), jnp.float32)
    wave_squared = jnp.clip(0.5 + 2.5 * jax.random.uniform(splits[2], (SUBS * GX, GY, GZ), jnp.float32) ** steps_of(splits[2], (SUBS * GX, GY, GZ), ((0, 32),), -0.2, 0.2), 0.5, 3.0)
    coupling_map = place_ends(jax.random.randint(splits[3], (SUBS, FACE), 0, ROWS_DEV), jax.random.fold_in(splits[3], 1), 0, ROWS_DEV - 1).astype(jnp.int32)
    front_rhs = gaussian(splits[4], (NRHS, ROWS), 1.0, 6.0, ((1, 8),), jnp.float32)
    row_order = jax.random.permutation(splits[5], ROWS).astype(jnp.int32)
    lower_panels = gaussian(splits[6], (W, ROWS), W ** -0.5, 0.125, ((1, 8),))
    inverse_slots = draw_inverse_slots(jax.random.fold_in(splits[9], 71), 0)
    panel_owners = draw_panel_owners(jax.random.fold_in(splits[9], 71), 0)
    return dict(leaf_field=leaf_field, leaf_source=leaf_source, wave_squared=wave_squared, coupling_map=coupling_map, front_rhs=front_rhs, row_order=row_order, lower_panels=lower_panels, inverse_slots=inverse_slots, panel_owners=panel_owners)


centre_weight = 128.0 / 30.0
face_weight = 14.0 / 30.0
cycle_weights = (0.0, 14.0 / 30.0, 3.0 / 30.0, 1.0 / 30.0)


def apply_operator(field, wave):
    lead = field.ndim - 3
    padded = jnp.pad(field, [(0, 0)] * lead + [(1, 1)] * 3)
    extent_x, extent_y, extent_z = field.shape[-3:]
    beside = jnp.zeros_like(field)
    for step_x in (-1, 0, 1):
        for step_y in (-1, 0, 1):
            for step_z in (-1, 0, 1):
                distance = abs(step_x) + abs(step_y) + abs(step_z)
                if distance == 0:
                    continue
                window = padded[..., 1 + step_x:1 + step_x + extent_x, 1 + step_y:1 + step_y + extent_y, 1 + step_z:1 + step_z + extent_z]
                beside = beside + cycle_weights[distance] * window
    return (centre_weight - wave) * field - beside


def reference(leaf_field, leaf_source, wave_squared, coupling_map, front_rhs, row_order, lower_panels, inverse_slots, panel_owners):
    field = leaf_field.reshape(NRHS, SUBS, GX, GY, GZ)
    source = leaf_source.reshape(NRHS, SUBS, GX, GY, GZ)
    wave = wave_squared.reshape(SUBS, GX, GY, GZ)
    residual = source - apply_operator(field, wave)
    leaf_residual = residual.reshape(NRHS, SUBS * GX, GY, GZ)
    face = residual[:, :, GX - 1].reshape(NRHS, SUBS * FACE)
    base = (jnp.arange(SUBS, dtype=jnp.int32) % BLOCKS) * ROWS_DEV
    targets = (base[:, None] + coupling_map.astype(jnp.int32)).reshape(-1)
    coupled = jax.ops.segment_sum(face_weight * face.T, targets, num_segments=ROWS).T
    reduced = front_rhs + coupled
    position = jnp.zeros((ROWS,), jnp.int32).at[row_order].set(jnp.arange(ROWS, dtype=jnp.int32))
    solved_list = []
    for panel in range(PANELS):
        block = jnp.take(reduced, position[panel * PW:(panel + 1) * PW], axis=1)
        start = (panel_owners[panel] * PW).astype(jnp.int32)
        inverse = lax.dynamic_slice_in_dim(inverse_slots, start, PW, 0)
        solved = lax.dot_general(block, inverse, (((1,), (1,)), ((), ())), precision=lax.Precision.HIGHEST, preferred_element_type=jnp.float32)
        solved_list.append(solved)
        solved_half = solved.astype(jnp.bfloat16)
        update = jnp.dot(solved_half, lower_panels[panel * PW:(panel + 1) * PW], preferred_element_type=jnp.float32)
        keep = (row_order >= (panel + 1) * PW).astype(jnp.float32)
        reduced = reduced - update * keep[None, :]
    return leaf_residual, jnp.concatenate(solved_list, axis=1), reduced
```

```python
import functools

import jax
import jax.numpy as jnp
from jax import lax
from jax.experimental import pallas as pl
from jax.experimental.pallas import tpu as pltpu
from jax.sharding import PartitionSpec as P

centre_weight = 128.0 / 30.0
face_weight = 14.0 / 30.0
edge_weight = 3.0 / 30.0
corner_weight = 1.0 / 30.0

VMEM = pl.BlockSpec(memory_space=pltpu.VMEM)
SMEM = pl.BlockSpec(memory_space=pltpu.SMEM)
F32 = jnp.float32
BF16 = jnp.bfloat16


def params():
    return pltpu.CompilerParams(vmem_limit_bytes=16 << 20)


def cost(flops, moved):
    return pl.CostEstimate(flops=flops, bytes_accessed=moved, transcendentals=0)


def dot_nt(a, b):
    return lax.dot_general(a, b, (((1,), (1,)), ((), ())), preferred_element_type=F32)


def split3(x):
    high = x.astype(BF16)
    rest = x - high.astype(F32)
    middle = rest.astype(BF16)
    low = (rest - middle.astype(F32)).astype(BF16)
    return high, middle, low


def select_columns(x, chosen):
    count = x.shape[0]
    parts = dot_nt(jnp.concatenate(split3(x), axis=0), chosen)
    return (parts[2 * count :] + parts[count : 2 * count]) + parts[:count]


def rows_of(index, size, total):
    return pl.ds(pl.multiple_of((index & (total // size - 1)) * size, 8), size)


def leaf_kernel(gx, gy, lanes, blocks, field, source, wave, cmap, residual, *rest):
    chunks, face, coupled = rest[:lanes], rest[lanes], rest[lanes + 1]
    step = pl.program_id(0)
    rows = field.shape[0]
    cells = gx * gy
    here = rows // cells
    width = field.shape[1]
    v = field[...]
    row = lax.broadcasted_iota(jnp.int32, (rows, width), 0) % cells
    lane = lax.broadcasted_iota(jnp.int32, (rows, width), 1)
    zero = jnp.zeros_like(v)
    left = jnp.where(lane > 0, pltpu.roll(v, 1, 1), zero)
    right = jnp.where(lane < width - 1, pltpu.roll(v, width - 1, 1), zero)
    sides = left + right
    once = face_weight * v + edge_weight * sides
    twice = edge_weight * v + corner_weight * sides
    y = row % gy

    def shift_y(p):
        below = jnp.where(y > 0, pltpu.roll(p, 1, 0), zero)
        above = jnp.where(y < gy - 1, pltpu.roll(p, rows - 1, 0), zero)
        return below + above

    around = once + shift_y(twice)
    below = jnp.where(row >= gy, pltpu.roll(around, gy, 0), zero)
    above = jnp.where(row < cells - gy, pltpu.roll(around, rows - gy, 0), zero)
    beside = face_weight * sides + shift_y(once) + (below + above)
    weight = centre_weight - wave[...]
    centre = (v.reshape(here, cells, width) * weight[None]).reshape(rows, width)
    residual[...] = source[...] - (centre - beside)
    for j in range(gy):
        face[pl.ds(step * here, here), j * width : (j + 1) * width] = residual[
            pl.ds(cells - gy + j, here, stride=cells), :
        ]

    @pl.when(step == blocks - 1)
    def _():
        slots = coupled.shape[1]
        hits = lax.broadcasted_iota(jnp.int32, (slots, cmap.shape[1]), 0) == cmap[...]
        coupled[...] = face_weight * select_columns(face[...], hits.astype(BF16))
        me = lax.axis_index("leaf")
        size = chunks[0].shape[0]
        for m in range(lanes):
            chunks[m][...] = coupled[rows_of(me ^ m, size, coupled.shape[0]), :]


def picker(order, panel, width):
    rows = order.shape[1]
    wanted = lax.broadcasted_iota(jnp.int32, (width, rows), 0) + panel * width
    return (wanted == order).astype(BF16)


def first_kernel(lanes, width, *refs):
    chunks, front, order, reduced, partial = refs[:lanes], *refs[lanes:]
    size = chunks[0].shape[0]
    total = front[rows_of(lax.axis_index("leaf"), size, front.shape[0]), :]
    for chunk in chunks:
        total = total + chunk[...]
    reduced[...] = total
    partial[...] = select_columns(total, picker(order[...], 0, width))


def split_kernel(inverse, high, middle, low):
    high[...], middle[...], low[...] = split3(inverse[...])


def solve_kernel(panel, a, b, high, middle, low, owners, out):
    block = a[...] + b[...]
    count = block.shape[0]
    bh, bm, bl = split3(block)
    first = dot_nt(jnp.concatenate([bh, bm, bl], axis=0), high[...])
    second = dot_nt(jnp.concatenate([bh, bm], axis=0), middle[...])
    third = dot_nt(bh, low[...])
    small = third + second[count:] + first[2 * count :]
    solved = (small + (second[:count] + first[count : 2 * count])) + first[:count]
    mine = owners[panel] == lax.axis_index("front")
    out[...] = jnp.where(mine, solved, jnp.zeros_like(solved))


def update_kernel(panel, last, a, b, lower, order, reduced_in, solved, reduced, *partial):
    width = a.shape[1]
    block = a[...] + b[...]
    solved[...] = block
    update = jnp.dot(block.astype(BF16), lower[...], preferred_element_type=F32)
    keep = order[...] >= (panel + 1) * width
    left = reduced_in[...] - jnp.where(keep, update, jnp.zeros_like(update))
    reduced[...] = left
    if not last:
        partial[0][...] = select_columns(left, picker(order[...], panel + 1, width))


def gather_kernel(groups, panels, *refs):
    solved_in, reduced_in = refs[: panels * groups], refs[panels * groups : (panels + 1) * groups]
    solved, reduced = refs[(panels + 1) * groups :]
    me = lax.axis_index("leaf")
    size, width = solved_in[0].shape
    for m in range(groups):
        rows = rows_of(me ^ m, size, solved.shape[0])
        reduced[rows, :] = reduced_in[m][...]
        for panel in range(panels):
            solved[rows, panel * width : (panel + 1) * width] = solved_in[panel * groups + m][...]


def per_device(
    lanes,
    fronts,
    leaf_field,
    leaf_source,
    wave_squared,
    coupling_map,
    front_rhs,
    row_order,
    lower_panels,
    inverse_slots,
    panel_owners,
):
    rhs_count, gx, gy, gz = leaf_field.shape
    cells = gx * gy
    rows_here = front_rhs.shape[1]
    width = inverse_slots.shape[1]
    panels = lower_panels.shape[0] // width
    groups = min(lanes, rhs_count // 8)
    share = rhs_count // groups

    def trade(x, axis, count, mask):
        return lax.ppermute(x, axis, [(i, i ^ mask) for i in range(count)])

    def butterfly(x):
        mask = 1
        while mask * 2 < fronts:
            if mask * 4 < fronts:
                r = [trade(x, "front", fronts, mask * k) for k in (3, 2, 1)]
                x = (x + r[2]) + (r[1] + r[0])
                mask *= 4
            else:
                x = x + trade(x, "front", fronts, mask)
                mask *= 2
        return x, trade(x, "front", fronts, mask)

    blocks = 4
    rows = rhs_count * cells
    field = leaf_field.reshape(rows, gz)
    source = leaf_source.reshape(rows, gz)
    wave = wave_squared.reshape(cells, gz)
    order = row_order.reshape(1, rows_here)
    piece = jax.ShapeDtypeStruct((share, rows_here), F32)
    tile = pl.BlockSpec((rows // blocks, gz), lambda i: (i, 0))
    whole = lambda shape: pl.BlockSpec(shape, lambda i: (0,) * len(shape))
    residual, *chunks = pl.pallas_call(
        functools.partial(leaf_kernel, gx, gy, lanes, blocks),
        grid=(blocks,),
        in_specs=[tile, tile, whole(wave.shape), whole(coupling_map.shape)],
        out_specs=[tile] + [whole(piece.shape)] * lanes,
        out_shape=[jax.ShapeDtypeStruct((rows, gz), F32)] + [piece] * lanes,
        scratch_shapes=[
            pltpu.VMEM((rhs_count, gy * gz), F32),
            pltpu.VMEM((rhs_count, rows_here), F32),
        ],
        compiler_params=params(),
        cost_estimate=cost(40 * rows * gz, 12 * rows * gz),
        name="leaf",
    )(field, source, wave, coupling_map)
    chunks = [chunks[0]] + [trade(chunks[m], "leaf", lanes, m) for m in range(1, lanes)]
    block_shape = jax.ShapeDtypeStruct((share, width), F32)
    reduced, partial = pl.pallas_call(
        functools.partial(first_kernel, lanes, width),
        in_specs=[VMEM] * (lanes + 2),
        out_specs=[VMEM, VMEM],
        out_shape=[piece, block_shape],
        compiler_params=params(),
        name="first",
    )(*chunks, front_rhs, order)
    pieces = pl.pallas_call(
        split_kernel,
        in_specs=[VMEM],
        out_specs=[VMEM] * 3,
        out_shape=[jax.ShapeDtypeStruct(inverse_slots.shape, BF16)] * 3,
        compiler_params=params(),
        name="split",
    )(inverse_slots)
    solved_list = []
    for panel in range(panels):
        last = panel == panels - 1
        a, b = butterfly(partial)
        own = pl.pallas_call(
            functools.partial(solve_kernel, panel),
            in_specs=[VMEM] * 5 + [SMEM],
            out_specs=VMEM,
            out_shape=block_shape,
            compiler_params=params(),
            name="solve",
        )(a, b, *pieces, panel_owners)
        a, b = butterfly(own)
        outs = pl.pallas_call(
            functools.partial(update_kernel, panel, last),
            in_specs=[VMEM] * 5,
            out_specs=[VMEM] * (2 if last else 3),
            out_shape=[block_shape, piece] + ([] if last else [block_shape]),
            compiler_params=params(),
            name="update",
        )(a, b, lower_panels[panel * width : (panel + 1) * width], order, reduced)
        solved, reduced = outs[:2]
        if not last:
            partial = outs[2]
        solved_list.append(solved)
    gathered = []
    for x in solved_list + [reduced]:
        gathered += [x] + [trade(x, "leaf", lanes, m) for m in range(1, groups)]
    solved, reduced = pl.pallas_call(
        functools.partial(gather_kernel, groups, panels),
        in_specs=[VMEM] * len(gathered),
        out_specs=[VMEM, VMEM],
        out_shape=[
            jax.ShapeDtypeStruct((rhs_count, panels * width), F32),
            jax.ShapeDtypeStruct((rhs_count, rows_here), F32),
        ],
        compiler_params=params(),
        name="collect",
    )(*gathered)
    return (residual.reshape(leaf_field.shape), solved, reduced)


def solution(mesh):
    return jax.shard_map(
        functools.partial(per_device, mesh.shape["leaf"], mesh.shape["front"]),
        mesh=mesh,
        in_specs=(
            P(None, ("leaf", "front"), None, None),
            P(None, ("leaf", "front"), None, None),
            P(("leaf", "front"), None, None),
            P(("leaf", "front"), None),
            P(None, "front"),
            P("front"),
            P(None, "front"),
            P("front", None),
            P(),
        ),
        out_specs=(P(None, ("leaf", "front"), None, None), P(), P(None, "front")),
        check_vma=False,
    )
```

```python
import functools

import jax
import jax.numpy as jnp
from jax import lax
from jax.experimental import pallas as pl
from jax.experimental.pallas import tpu as pltpu
from jax.sharding import PartitionSpec as P

centre_weight = 128.0 / 30.0
face_weight = 14.0 / 30.0
edge_weight = 3.0 / 30.0
corner_weight = 1.0 / 30.0

VMEM = pl.BlockSpec(memory_space=pltpu.VMEM)
SMEM = pl.BlockSpec(memory_space=pltpu.SMEM)
F32 = jnp.float32
BF16 = jnp.bfloat16


def params():
    return pltpu.CompilerParams(vmem_limit_bytes=16 << 20)


def cost(flops, moved):
    return pl.CostEstimate(flops=flops, bytes_accessed=moved, transcendentals=0)


def dot_nt(a, b):
    return lax.dot_general(a, b, (((1,), (1,)), ((), ())), preferred_element_type=F32)


def split3(x):
    high = x.astype(BF16)
    rest = x - high.astype(F32)
    middle = rest.astype(BF16)
    low = (rest - middle.astype(F32)).astype(BF16)
    return high, middle, low


def split2(x):
    high = x.astype(BF16)
    return high, (x - high.astype(F32)).astype(BF16)


def select_columns(x, chosen):
    count = x.shape[0]
    parts = dot_nt(jnp.concatenate(split3(x), axis=0), chosen)
    return (parts[2 * count :] + parts[count : 2 * count]) + parts[:count]


def rows_of(index, size, total):
    return pl.ds(pl.multiple_of((index & (total // size - 1)) * size, 8), size)


def leaf_kernel(gx, gy, lanes, blocks, field, source, wave, cmap, front, residual, *rest):
    chunks, face, coupled = rest[:lanes], rest[lanes], rest[lanes + 1]
    step = pl.program_id(0)
    rows = field.shape[0]
    cells = gx * gy
    here = rows // cells
    width = field.shape[1]
    v = field[...]
    row = lax.broadcasted_iota(jnp.int32, (rows, width), 0) % cells
    lane = lax.broadcasted_iota(jnp.int32, (rows, width), 1)
    zero = jnp.zeros_like(v)
    left = jnp.where(lane > 0, pltpu.roll(v, 1, 1), zero)
    right = jnp.where(lane < width - 1, pltpu.roll(v, width - 1, 1), zero)
    sides = left + right
    once = face_weight * v + edge_weight * sides
    twice = edge_weight * v + corner_weight * sides
    y = row % gy

    def shift_y(p):
        below = jnp.where(y > 0, pltpu.roll(p, 1, 0), zero)
        above = jnp.where(y < gy - 1, pltpu.roll(p, rows - 1, 0), zero)
        return below + above

    around = once + shift_y(twice)
    below = jnp.where(row >= gy, pltpu.roll(around, gy, 0), zero)
    above = jnp.where(row < cells - gy, pltpu.roll(around, rows - gy, 0), zero)
    beside = face_weight * sides + shift_y(once) + (below + above)
    weight = centre_weight - wave[...]
    centre = (v.reshape(here, cells, width) * weight[None]).reshape(rows, width)
    residual[...] = source[...] - (centre - beside)
    for j in range(gy):
        face[pl.ds(step * here, here), j * width : (j + 1) * width] = residual[
            pl.ds(cells - gy + j, here, stride=cells), :
        ]

    @pl.when(step == blocks - 1)
    def _():
        slots = coupled.shape[1]
        hits = lax.broadcasted_iota(jnp.int32, (slots, cmap.shape[1]), 0) == cmap[...]
        coupled[...] = face_weight * select_columns(face[...], hits.astype(BF16))
        me = lax.axis_index("leaf")
        size = chunks[0].shape[0]
        for m in range(lanes):
            rows_there = rows_of(me ^ m, size, coupled.shape[0])
            chunk = coupled[rows_there, :]
            chunks[m][...] = chunk if m else chunk + front[rows_there, :]


def picker(order, panel, width):
    rows = order.shape[1]
    wanted = lax.broadcasted_iota(jnp.int32, (width, rows), 0) + panel * width
    return (wanted == order).astype(BF16)


def prelude_kernel(quarters, panels, inverse, lower, order, slot, under, held, sems):
    width = inverse.shape[1]
    size = width // quarters
    start = (lax.axis_index("leaf") & (quarters - 1)) * size
    copies = [pltpu.make_async_copy(inverse.at[pl.ds(pl.multiple_of(start, size), size), :], slot, sems.at[0])]
    for panel in range(panels - 1):
        rows = pl.ds(pl.multiple_of(panel * width + start, size), size)
        copies.append(pltpu.make_async_copy(lower.at[rows, :], held.at[panel], sems.at[panel + 1]))
    for copy in copies:
        copy.start()
    own = order[...]
    under[size:, :] = jnp.broadcast_to(own.astype(F32), (8, own.shape[1]))
    total = jnp.zeros(held.shape[1:], F32)
    for panel in range(panels - 1):
        copies[panel + 1].wait()
        here = (own >= (panel + 1) * width) & (own < (panel + 2) * width)
        total = total + jnp.where(here, held[panel].astype(F32), jnp.zeros_like(total))
    under[:size, :] = total
    copies[0].wait()


def pack_kernel(*refs):
    out = refs[-1]
    width = refs[0].shape[1]
    for i, piece in enumerate(refs[:-1]):
        out[:, i * width : (i + 1) * width] = piece[: out.shape[0], :]


def under_kernel(*refs):
    pieces, out = refs[:-1], refs[-1]
    size = pieces[0].shape[0]
    me = lax.axis_index("leaf") & (len(pieces) - 1)
    for k, piece in enumerate(pieces):
        out[pl.ds(pl.multiple_of((me ^ k) * size, size), size), :] = piece[...].astype(BF16)


def slots_kernel(quarters, inverse, *refs):
    pieces, (high, middle) = refs[:-2], refs[-2:]
    me = lax.axis_index("leaf") & (quarters - 1)
    high[0], middle[0] = split2(inverse[...])
    for i, piece in enumerate(pieces):
        size = piece.shape[0]
        rows = pl.ds(pl.multiple_of((me ^ (i % quarters)) * size, size), size)
        high[i // quarters + 1, rows, :], middle[i // quarters + 1, rows, :] = split2(piece[...])


def first_kernel(*refs):
    chunks, reduced = refs[:-1], refs[-1]
    total = chunks[0][...]
    for chunk in chunks[1:]:
        total = total + chunk[...]
    reduced[...] = total


def solve_share(panel, near, rows, orders, high, middle, owners, out):
    count = rows.shape[0]
    width = out.shape[1]
    wanted = lax.broadcasted_iota(jnp.int32, (width, orders.shape[1]), 0) + panel * width
    chosen = (wanted == orders).astype(BF16)
    block = dot_nt(jnp.concatenate(split2(rows), axis=0), chosen).astype(BF16)
    apart = owners[panel] ^ lax.axis_index("front")
    slot = apart // near
    first = dot_nt(block, high[slot])
    second = dot_nt(block[:count], middle[slot])
    solved = (second + first[count:]) + first[:count]
    holds = (apart & (near - 1)) == 0
    out[...] = jnp.where(holds, solved, jnp.zeros_like(solved))


def begin_kernel(near, size, *refs):
    rows, own, under = refs[:near], refs[near], refs[near + 1 : 2 * near]
    high, middle, owners, orders, out = refs[2 * near :]
    orders[...] = jnp.concatenate(
        [own[...]] + [x[size : size + 1, :].astype(jnp.int32) for x in under], axis=1
    )
    values = jnp.concatenate([x[...] for x in rows], axis=1)
    solve_share(0, near, values, orders[...], high, middle, owners, out)


def join_kernel(a, b, reduced, out):
    width = a.shape[1]
    out[:, :width] = a[...] + b[...]
    out[:, width:] = reduced[...]


def updated(panel, half, lower, order, reduced):
    update = jnp.dot(half, lower[...], preferred_element_type=F32)
    keep = order >= (panel + 1) * half.shape[1]
    return reduced[...] - jnp.where(keep, update, jnp.zeros_like(update))


def step_kernel(panel, near, loose, *refs):
    parts, refs = refs[:near], refs[near:]
    others, refs = refs[:loose], refs[loose:]
    lower, below, orders, reduced_in, high, middle, owners = refs[:7]
    earlier, (solved, reduced, out) = refs[7:-3], refs[-3:]
    width = out.shape[1]
    rows_here = reduced.shape[1]
    p = [x[:, :width] for x in parts]
    block = (p[0] + p[1]) + (p[2] + p[3])
    for i, x in enumerate(earlier):
        solved[:, i * width : (i + 1) * width] = x[...]
    solved[:, len(earlier) * width :] = block
    half = block.astype(BF16)
    left = updated(panel, half, lower, orders[:, :rows_here], reduced_in)
    reduced[...] = left
    values = [x[...] for x in others] if loose else [x[:, width:] for x in parts[1:]]
    values = jnp.concatenate(values, axis=1)
    values = values - jnp.dot(half, below[...], preferred_element_type=F32)
    rows = jnp.concatenate([left, values], axis=1)
    solve_share(panel + 1, near, rows, orders[...], high, middle, owners, out)


def last_kernel(panel, near, *refs):
    parts, lower, orders, reduced_in, out = refs[:near], *refs[near : near + 3], refs[-1]
    width = lower.shape[0]
    p = [x[:, :width] for x in parts]
    block = (p[0] + p[1]) + (p[2] + p[3])
    out[:, :width] = block
    out[:, width:] = updated(panel, block.astype(BF16), lower, orders[:, : out.shape[1] - width], reduced_in)


def gather_kernel(groups, *refs):
    early, late = refs[:groups], refs[groups : 2 * groups]
    solved, reduced = refs[2 * groups :]
    me = lax.axis_index("leaf")
    size, ahead = early[0].shape
    width = solved.shape[1] - ahead
    for m in range(groups):
        rows = rows_of(me ^ m, size, solved.shape[0])
        solved[rows, :ahead] = early[m][...]
        solved[rows, ahead:] = late[m][:, :width]
        reduced[rows, :] = late[m][:, width:]


def per_device(
    lanes,
    fronts,
    leaf_field,
    leaf_source,
    wave_squared,
    coupling_map,
    front_rhs,
    row_order,
    lower_panels,
    inverse_slots,
    panel_owners,
):
    rhs_count, gx, gy, gz = leaf_field.shape
    cells = gx * gy
    rows_here = front_rhs.shape[1]
    width = inverse_slots.shape[1]
    panels = lower_panels.shape[0] // width
    groups = min(lanes, rhs_count // 8)
    share = rhs_count // groups

    near, quarters = 4, 4
    far = fronts // near

    def trade(x, axis, count, mask):
        return lax.ppermute(x, axis, [(i, i ^ mask) for i in range(count)])

    def across(x):
        mask = near
        while mask * 2 < fronts:
            x = x + trade(x, "front", fronts, mask)
            mask *= 2
        return x, trade(x, "front", fronts, mask)

    def nearby(x):
        r = {m: trade(x, "front", fronts, m) for m in reversed(range(1, near))}
        return [x] + [r[m] for m in range(1, near)]

    def call(kernel, name, operands, out_shape, in_specs=None, **kw):
        many = isinstance(out_shape, list)
        return pl.pallas_call(
            kernel,
            in_specs=in_specs or [VMEM] * len(operands),
            out_specs=[VMEM] * len(out_shape) if many else VMEM,
            out_shape=out_shape,
            compiler_params=kw.pop("compiler_params", params()),
            name=name,
            **kw,
        )(*operands)

    def f32(*shape):
        return jax.ShapeDtypeStruct(shape, F32)

    def bf16(*shape):
        return jax.ShapeDtypeStruct(shape, BF16)

    blocks = 4
    rows = rhs_count * cells
    field = leaf_field.reshape(rows, gz)
    source = leaf_source.reshape(rows, gz)
    wave = wave_squared.reshape(cells, gz)
    order = row_order.reshape(1, rows_here)
    size = width // quarters
    anywhere = pl.BlockSpec(memory_space=pl.ANY)

    slot, under = call(
        functools.partial(prelude_kernel, quarters, panels),
        "prelude",
        (inverse_slots, lower_panels, order),
        [f32(size, width), f32(size + 8, rows_here)],
        [anywhere, anywhere, VMEM],
        scratch_shapes=[
            pltpu.VMEM((panels - 1, size, rows_here), BF16),
            pltpu.SemaphoreType.DMA((panels,)),
        ],
        compiler_params=None,
    )
    slots = [trade(slot, "front", fronts, near * m) for m in range(1, far)]
    unders = nearby(under)[1:]

    piece, block_shape = f32(share, rows_here), f32(share, width)
    tile = pl.BlockSpec((rows // blocks, gz), lambda i: (i, 0))
    whole = lambda shape: pl.BlockSpec(shape, lambda i: (0,) * len(shape))
    residual, *chunks = pl.pallas_call(
        functools.partial(leaf_kernel, gx, gy, lanes, blocks),
        grid=(blocks,),
        in_specs=[tile, tile] + [whole(x.shape) for x in (wave, coupling_map, front_rhs)],
        out_specs=[tile] + [whole(piece.shape)] * lanes,
        out_shape=[f32(rows, gz)] + [piece] * lanes,
        scratch_shapes=[
            pltpu.VMEM((rhs_count, gy * gz), F32),
            pltpu.VMEM((rhs_count, rows_here), F32),
        ],
        compiler_params=params(),
        cost_estimate=cost(40 * rows * gz, 12 * rows * gz),
        name="leaf",
    )(field, source, wave, coupling_map, front_rhs)
    chunks = [chunks[0]] + [trade(chunks[m], "leaf", lanes, m) for m in range(1, lanes)]
    reduced = call(first_kernel, "first", chunks, piece)
    groups_rows = nearby(reduced)

    def all_quarters(x):
        y = trade(x, "leaf", lanes, 2)
        return [x, trade(x, "leaf", lanes, 1), y, trade(y, "leaf", lanes, 1)]

    pieces = [q for x in slots for q in all_quarters(x)]
    high, middle = call(
        functools.partial(slots_kernel, quarters),
        "slots",
        (inverse_slots, *pieces),
        [bf16(far, *inverse_slots.shape)] * 2,
    )
    packed = call(pack_kernel, "pack", unders, f32(size, (near - 1) * rows_here))
    below = call(under_kernel, "under", all_quarters(packed), bf16(width, (near - 1) * rows_here))

    orders, own = call(
        functools.partial(begin_kernel, near, size),
        "begin",
        (*groups_rows, order, *unders, high, middle, panel_owners),
        [jax.ShapeDtypeStruct((1, near * rows_here), jnp.int32), block_shape],
        [VMEM] * (2 * near + 2) + [SMEM],
    )
    solved_list, early = [], []
    for panel in range(panels):
        lower = lower_panels[panel * width : (panel + 1) * width]
        a, b = across(own)
        if panel == 0:
            parts, loose = nearby(a + b), groups_rows[1:]
        else:
            joined = call(join_kernel, "join", (a, b, reduced), f32(share, width + rows_here))
            parts, loose = nearby(joined), []
        if panel == panels - 1:
            late = call(
                functools.partial(last_kernel, panel, near),
                "last",
                (*parts, lower, orders, reduced, *early[1:]),
                f32(share, width + rows_here),
                [VMEM] * (near + 3) + [anywhere] * len(early[1:]),
            )
            continue
        pack = panel == panels - 2
        earlier = solved_list if pack else []
        operands = (*parts, *loose, lower, below, orders, reduced, high, middle)
        solved, reduced, own = call(
            functools.partial(step_kernel, panel, near, len(loose)),
            "step",
            (*operands, panel_owners, *earlier),
            [f32(share, width * (len(earlier) + 1)), piece, block_shape],
            [VMEM] * len(operands) + [SMEM] + [VMEM] * len(earlier),
        )
        solved_list.append(solved)
        if pack:
            early = [solved] + [trade(solved, "leaf", lanes, m) for m in range(1, groups)]
    late = [late] + [trade(late, "leaf", lanes, m) for m in range(1, groups)]
    solved, reduced = call(
        functools.partial(gather_kernel, groups),
        "collect",
        (*early, *late),
        [f32(rhs_count, panels * width), f32(rhs_count, rows_here)],
    )
    return (residual.reshape(leaf_field.shape), solved, reduced)


def solution(mesh):
    return jax.shard_map(
        functools.partial(per_device, mesh.shape["leaf"], mesh.shape["front"]),
        mesh=mesh,
        in_specs=(
            P(None, ("leaf", "front"), None, None),
            P(None, ("leaf", "front"), None, None),
            P(("leaf", "front"), None, None),
            P(("leaf", "front"), None),
            P(None, "front"),
            P("front"),
            P(None, "front"),
            P("front", None),
            P(),
        ),
        out_specs=(P(None, ("leaf", "front"), None, None), P(), P(None, "front")),
        check_vma=False,
    )
```
